128 devices in a mesh: lat: 8 (over x, core), lon: 16 (over z, y).
Axes of the slice: x: 4, y: 4, z: 4, core: 2. Of those that a mesh axis runs over, the one named last changes fastest.
Arguments:
- obs_value: float32 [128, 21, 128, 128], P(('lat', 'lon')), may hold values from -6 to 6
- obs_cell: int32 [128, 128, 128], P(('lat', 'lon')), may hold values from 0 to 12287
- obs_count: int32 [128, 128], P(('lat', 'lon')), may hold values from 0 to 128, as said below
- bottom_level: int32 [384, 4096], P('lat', 'lon'), may hold values from 0 to 10
- diffusivity: float32 [2, 384, 4096], P(None, 'lat', 'lon'), may hold values from 0.5 to 16
- partner: int32 [4096], P('lon'), may hold values from 0 to 4095, as said below
- length_scale: float32 [21], replicated, may hold values from 0.25 to 2
- sigma: float32 [21], replicated, may hold values from 0.5 to 2
Outputs:
- obs_fit: float32 [128, 21, 128, 128], P(('lat', 'lon'))
- diffused: float32 [21, 384, 4096], P(None, 'lat', 'lon')
The draws below stay inside these ranges and needn't reach their ends.
Inputs may be any that keep to these rules, and one draw needn't show every extreme that they name: `obs_count`: at most 128 live slots from one device to one owner; in every draw one owner receives 128 from every device. partner[i] = (centre - i) mod 4096 for one centre of each draw.
All inputs are finite; a program needn't handle non-finite values.
Results may differ from the reference program's by a relative error of at most 0.00002.
Values sent between devices are 32-bit elements; how exact they have to be, the bound alone decides.
A program may use at most 128 MiB of HBM per device.

```python
import math
import jax
import jax.numpy as jnp

LEV = 10
STEPS = 2
SWEEPS = 6
CLAT = 48
CLON = 256
CAP = 128
C = 21
NLAT = 384
NLON = 4096
N_LON = 16
DEVICES = 128


def draw_obs_count(key, part):
    key_dense, key_raw, key_full = jax.random.split(key, 3)
    density = jax.random.randint(key_dense, (DEVICES,), 1, 9)
    ceiling = CAP * density[None, :] // 4 + 1
    raw_counts = jax.random.randint(key_raw, (DEVICES, DEVICES), 0, ceiling)
    counts = jnp.minimum(raw_counts, CAP)
    full_owner = jax.random.randint(key_full, (), 0, DEVICES)
    owners = jnp.arange(DEVICES, dtype=jnp.int32)[None, :]
    return jnp.where(owners == full_owner, CAP, counts).astype(jnp.int32)


def draw_partner(key, part):
    centre = jax.random.randint(key, (), 0, NLON)
    return jnp.mod(centre - jnp.arange(NLON, dtype=jnp.int32), NLON).astype(jnp.int32)


def place_ends(array, rng, least, largest):
    place = [jax.random.randint(jax.random.fold_in(rng, axis), (), 0, length) for axis, length in enumerate(array.shape)]
    widest = array.shape.index(max(array.shape))
    beside = place[:widest] + [(place[widest] + 1) % array.shape[widest]] + place[widest + 1:]
    return array.at[tuple(place)].set(least).at[tuple(beside)].set(largest)


def levels(rng, extent, pieces, least, high):
    loudness = 1.0
    for position, parts in pieces:
        steps = jax.random.uniform(jax.random.fold_in(jax.random.fold_in(rng, 6), position), (parts,), jnp.float32, least / len(pieces), high / len(pieces))
        loudness = loudness * jnp.repeat(jnp.exp(steps), extent[position] // parts).reshape((-1,) + (1,) * (len(extent) - 1 - position))
    return loudness


def gaussian(key, shape, deviation, limit, shards=(), kind=jnp.bfloat16):
    values = jax.random.normal(key, shape, jnp.float32) * deviation
    if len(shards) > 0:
        values = levels(key, shape, shards, -0.22, 0.18) * values
    return jnp.clip(values, min=-limit, max=limit).astype(kind)


def setup_inputs(seed: int = 0) -> dict:
    arg_keys = jax.random.split(jax.random.key(seed), 9)
    obs_value = gaussian(arg_keys[0], (DEVICES, C, DEVICES, CAP), 1.0, 6.0, ((0, 128),), jnp.float32)
    obs_cell = place_ends(jax.random.randint(arg_keys[1], (DEVICES, DEVICES, CAP), 0, CLAT * CLON), jax.random.fold_in(arg_keys[1], 1), 0, (CLAT * CLON) - 1).astype(jnp.int32)
    obs_count = draw_obs_count(jax.random.fold_in(arg_keys[8], 71), 0)
    bottom_level = place_ends(jax.random.randint(arg_keys[3], (NLAT, NLON), 0, LEV + 1), jax.random.fold_in(arg_keys[3], 1), 0, LEV).astype(jnp.int32)
    diffusivity = jnp.clip(jnp.exp(math.log(16.0) - 3.465736 * jax.random.uniform(arg_keys[4], (2, NLAT, NLON), jnp.float32) ** levels(arg_keys[4], (2, NLAT, NLON), ((1, 8), (2, 16)), -0.2, 0.2)), 0.5, 16.0)
    partner = draw_partner(jax.random.fold_in(arg_keys[8], 71), 0)
    length_scale = jnp.clip(jnp.exp(jax.random.uniform(arg_keys[6], (C,), jnp.float32, math.log(0.25), math.log(2.0))), 0.25, 2.0)
    sigma = jnp.clip(jnp.exp(jax.random.uniform(arg_keys[7], (C,), jnp.float32, math.log(0.5), math.log(2.0))), 0.5, 2.0)
    return dict(obs_value=obs_value, obs_cell=obs_cell, obs_count=obs_count, bottom_level=bottom_level, diffusivity=diffusivity, partner=partner, length_scale=length_scale, sigma=sigma)


def level_table():
    return jnp.concatenate([jnp.arange(LEV, dtype=jnp.int32), jnp.arange(LEV, dtype=jnp.int32), jnp.zeros((1,), jnp.int32)])


def neighbours(block, partner):
    east = jnp.roll(block, -1, axis=2)
    west = jnp.roll(block, 1, axis=2)
    north = jnp.concatenate([block[:, 1:], block[:, -1:][:, :, partner]], axis=1)
    south = jnp.concatenate([jnp.zeros_like(block[:, :1]), block[:, :-1]], axis=1)
    return east, west, north, south


def reference(obs_value, obs_cell, obs_count, bottom_level, diffusivity, partner, length_scale, sigma):
    channels = 2 * LEV + 1
    wet_mask = (level_table()[:, None, None] < bottom_level[None]).astype(jnp.float32)
    live_slots = (jnp.arange(CAP, dtype=jnp.int32)[None, None, :] < obs_count[:, :, None]).astype(jnp.float32)
    values = obs_value * live_slots[:, None, :, :]
    owners = jnp.arange(DEVICES, dtype=jnp.int32)
    first_row = (owners // N_LON) * CLAT
    first_col = (owners % N_LON) * CLON
    rows_global = first_row[None, :, None] + obs_cell // CLON
    cols_global = first_col[None, :, None] + obs_cell % CLON
    flat_cells = (rows_global * NLON + cols_global).reshape(-1).astype(jnp.int32)
    spread = jnp.transpose(values, (1, 0, 2, 3)).reshape(channels, -1)
    field = jnp.zeros((channels, NLAT * NLON), jnp.float32).at[:, flat_cells].add(spread)
    field = field.reshape(channels, NLAT, NLON) * (sigma[:, None, None] * wet_mask)
    scale = length_scale[:, None, None]
    wet_e, wet_w, wet_n, wet_s = neighbours(wet_mask, partner)
    lon_e, lon_w, unused_n, unused_s = neighbours(diffusivity[0][None], partner)
    unused_e, unused_w, lat_n, lat_s = neighbours(diffusivity[1][None], partner)
    kappa_lon = diffusivity[0][None]
    kappa_lat = diffusivity[1][None]
    w_east = scale * (0.5 * (kappa_lon + lon_e)) * wet_mask * wet_e
    w_west = scale * (0.5 * (kappa_lon + lon_w)) * wet_mask * wet_w
    w_north = scale * (0.5 * (kappa_lat + lat_n)) * wet_mask * wet_n
    w_south = scale * (0.5 * (kappa_lat + lat_s)) * wet_mask * wet_s
    diagonal_sum = 1.0 + w_east + w_west + w_north + w_south
    state = field
    for step_index in range(STEPS):
        source = state
        for sweep_index in range(SWEEPS):
            east, west, north, south = neighbours(state, partner)
            state = (source + w_east * east + w_west * west + w_north * north + w_south * south) / diagonal_sum
    diffused = sigma[:, None, None] * state
    fits = diffused.reshape(channels, -1)[:, flat_cells].reshape(channels, DEVICES, DEVICES, CAP)
    obs_fit = jnp.transpose(fits, (1, 0, 2, 3)) * live_slots[:, None, :, :]
    return obs_fit, diffused
```

```python
import functools

import jax
import jax.numpy as jnp
from jax import lax
from jax.experimental import pallas as pl
from jax.experimental.pallas import tpu as pltpu
from jax.sharding import PartitionSpec as P

LEV = 10
C = 21
CP = 24
ROWS = 48
COLS = 256
BAND = ROWS // 2
PLACES = 2 * COLS
DEEP = 12
EXT = ROWS + 2 * DEEP
GRP = 16
CEXT = ROWS + 2 * GRP
F32 = jnp.float32
BF16 = jnp.bfloat16
MESH = pl.DeviceIdType.MESH
VMEM_LIMIT = 60 * 2**20


def place_of(linear, n_lon):
    return (linear // n_lon, lax.rem(linear, n_lon))


def split(cell):
    cell = cell.astype(jnp.int32)
    place = cell & (PLACES - 1)
    low = place & 255
    half = place >> 8
    return cell >> 9, [jnp.where(half == h, low, 512).astype(F32) for h in range(2)]


def store_onehot(onehot, halves, lanes):
    one = jnp.ones((16, 128), BF16)
    zero = jnp.zeros((16, 128), BF16)
    steps = lax.broadcasted_iota(jnp.int32, (16, 128), 0).astype(F32).astype(BF16)
    for h in range(2):
        row = jnp.broadcast_to(halves[h], (16, 128)).astype(BF16)
        for t in range(16):
            first = h * 256 + t * 16
            onehot[first : first + 16, lanes] = jnp.where(row == steps + BF16(16 * t), one, zero)


def build_chunk(arrived, chunk, size, lhs, onehot):
    for j in range(size):
        value = arrived[chunk * size + j]
        band, halves = split(value[C : C + 1, :])
        lanes = slice(j * 128, (j + 1) * 128)
        high = value.astype(BF16)
        pieces = jnp.concatenate([value, value - high.astype(F32)], axis=0).astype(BF16)
        band = jnp.broadcast_to(band.astype(F32), (16, 128)).astype(BF16)
        zero = jnp.zeros((2 * CP, 128), BF16)
        for b in range(BAND):
            mask = jnp.concatenate([band == BF16(b)] * 3, axis=0)
            lhs[b * 2 * CP : (b + 1) * 2 * CP, lanes] = jnp.where(mask, pieces, zero)
        store_onehot(onehot, halves, lanes)


def scatter_kernel(
    n, n_lon, size, value_ref, cell_ref, field_ref, slot_ref,
    outgoing, arrived, lhs0, onehot0, lhs1, onehot1, total, local_sem, send_sem, recv_sem,
):
    me = lax.axis_index("lat") * n_lon + lax.axis_index("lon")
    load = pltpu.make_async_copy(value_ref, outgoing.at[0:C], local_sem.at[0])
    load.start()
    barrier = pltpu.get_barrier_semaphore()

    def greet(i, carry):
        pl.semaphore_signal(barrier, inc=1, device_id=place_of(lax.rem(me + i, n), n_lon), device_id_type=MESH)
        return carry

    lax.fori_loop(1, n, greet, 0)
    outgoing[C] = cell_ref[...]
    total[...] = jnp.zeros_like(total)
    load.wait()
    pl.semaphore_wait(barrier, n - 1)

    def send(i, carry):
        owner = lax.rem(me + i, n)
        pltpu.make_async_remote_copy(
            src_ref=outgoing.at[:, owner, :],
            dst_ref=arrived.at[i, 0 : C + 1, :],
            send_sem=send_sem,
            recv_sem=recv_sem.at[i // size],
            device_id=place_of(owner, n_lon),
            device_id_type=MESH,
        ).start()
        return carry

    own = pltpu.make_async_copy(outgoing.at[:, me, :], arrived.at[0, 0 : C + 1, :], local_sem.at[1])
    own.start()
    lax.fori_loop(1, n, send, 0)
    own.wait()

    def arrive(chunk, first):
        window = arrived.at[pl.ds(chunk * size + first, size - first), 0 : C + 1, :]
        pltpu.make_async_copy(window, window, recv_sem.at[chunk]).wait()

    chunks = n // size
    dims = (((1,), (1,)), ((), ()))
    arrive(0, 1)
    build_chunk(arrived, 0, size, lhs0, onehot0)

    def pair(i, carry):
        arrive(2 * i + 1, 0)
        build_chunk(arrived, 2 * i + 1, size, lhs1, onehot1)
        total[...] += lax.dot_general(lhs0[...], onehot0[...], dims, preferred_element_type=F32)
        more = 2 * i + 2

        @pl.when(more < chunks)
        def _():
            arrive(more, 0)

        build_chunk(arrived, jnp.minimum(more, chunks - 1), size, lhs0, onehot0)
        total[...] += lax.dot_general(lhs1[...], onehot1[...], dims, preferred_element_type=F32)
        return carry

    lax.fori_loop(0, chunks // 2, pair, 0)
    for b in range(BAND):
        first = b * 2 * CP
        band = total[first : first + CP, :] + total[first + CP : first + 2 * CP, :]
        for t in range(4):
            field_ref[t % 2, 2 * b + t // 2] = band[:, t * 128 : (t + 1) * 128]
    slot_ref[...] = arrived[:, C, :]
    sent = arrived.at[1:n, 0 : C + 1, :]
    pltpu.make_async_copy(sent, sent, send_sem).wait()


def scatter(n, n_lon, value, cell):
    size = min(8, n // 4)
    vmem = pl.BlockSpec(memory_space=pltpu.VMEM)
    buffers = [
        pltpu.VMEM((BAND * 2 * CP, size * 128), BF16),
        pltpu.VMEM((PLACES, size * 128), BF16),
    ]
    return pl.pallas_call(
        functools.partial(scatter_kernel, n, n_lon, size),
        out_shape=(
            jax.ShapeDtypeStruct((2, ROWS, CP, 128), F32),
            jax.ShapeDtypeStruct((n, 128), F32),
        ),
        in_specs=[pl.BlockSpec(memory_space=pl.ANY), vmem],
        out_specs=(vmem, vmem),
        scratch_shapes=[
            pltpu.VMEM((C + 1, n, 128), F32),
            pltpu.VMEM((n, CP, 128), F32),
            *buffers,
            *buffers,
            pltpu.VMEM((BAND * 2 * CP, PLACES), F32),
            pltpu.SemaphoreType.DMA((2,)),
            pltpu.SemaphoreType.DMA,
            pltpu.SemaphoreType.DMA((n // size,)),
        ],
        compiler_params=pltpu.CompilerParams(
            collective_id=0, has_side_effects=True, vmem_limit_bytes=VMEM_LIMIT
        ),
        name="scatter",
    )(value, cell)


def lanes_of(shape):
    return lax.broadcasted_iota(jnp.int32, shape, len(shape) - 1)


def east_of(tiles):
    turned = [pltpu.roll(x, 127, x.ndim - 1) for x in tiles]
    last = lanes_of(tiles[0].shape) == 127
    return [jnp.where(last, turned[(t + 1) % 3], turned[t]) for t in range(3)]


def west_of(tiles):
    turned = [pltpu.roll(x, 1, x.ndim - 1) for x in tiles]
    first = lanes_of(tiles[0].shape) == 0
    return [jnp.where(first, turned[(t + 2) % 3], turned[t]) for t in range(3)]


def diffuse_kernel(
    n_lat, n_lon, partner_ref, field_ref, coef_ref, scale_ref, sigma_ref, out_ref,
    cur, nxt, rhs, inv, w_e, w_w, w_n, w_s, pack_e, pack_w, edge_e, edge_w,
    coef, coef_e, coef_w, fold, coef_fold, send_sem, recv_sem, fold_send, fold_recv, local_sem,
):
    lat = lax.axis_index("lat")
    lon = lax.axis_index("lon")
    east = lax.rem(lon + 1, n_lon)
    west = lax.rem(lon + n_lon - 1, n_lon)
    has_n = lat < n_lat - 1
    has_s = lat > 0
    top = lat == n_lat - 1
    everywhere = lat >= 0
    north = jnp.minimum(lat + 1, n_lat - 1)
    south = jnp.maximum(lat - 1, 0)
    ways = [
        (everywhere, lat, east, everywhere),
        (everywhere, lat, west, everywhere),
        (has_n, north, lon, has_s),
        (has_s, south, lon, has_n),
        (has_n, north, east, has_s),
        (has_n, north, west, has_s),
        (has_s, south, east, has_n),
        (has_s, south, west, has_n),
    ]
    barrier = pltpu.get_barrier_semaphore()
    for exists, to_lat, to_lon, _ in ways:
        @pl.when(exists)
        def _():
            pl.semaphore_signal(barrier, inc=1, device_id=(to_lat, to_lon), device_id_type=MESH)

    def greet(i, carry):
        pl.semaphore_signal(barrier, inc=1, device_id=(lat, lax.rem(lon + i, n_lon)), device_id_type=MESH)
        return carry

    @pl.when(top)
    def _():
        lax.fori_loop(1, n_lon, greet, 0)

    lane16 = lanes_of((CP, 128)) >> 4
    for i in range(ROWS // 8):
        first = jnp.zeros((CP, 128), F32)
        last = jnp.zeros((CP, 128), F32)
        for j in range(8):
            x = field_ref[0, 8 * i + j]
            y = field_ref[1, 8 * i + j]
            first = jnp.where(lane16 == j, pltpu.roll(x, 16 * j, 1) if j else x, first)
            last = jnp.where(lane16 == j, pltpu.roll(y, 16 * j + 16, 1) if j < 7 else y, last)
        pack_w[i] = first
        pack_e[i] = last

    @pl.when(lat == 0)
    def _():
        cur[0:2, 0:DEEP] = jnp.zeros((2, DEEP, CP, 128), F32)
        edge_e[0:2] = jnp.zeros((2, CP, 128), F32)
        edge_w[0:2] = jnp.zeros((2, CP, 128), F32)
        coef[:, :, 0:GRP, :] = jnp.zeros((2, 3, GRP, 128), F32)
        coef_e[:, 0:GRP, :] = jnp.zeros((3, GRP, 128), F32)
        coef_w[:, 0:GRP, :] = jnp.zeros((3, GRP, 128), F32)

    @pl.when(top)
    def _():
        edge_e[8:10] = jnp.zeros((2, CP, 128), F32)
        edge_w[8:10] = jnp.zeros((2, CP, 128), F32)
        coef_e[:, GRP + ROWS : CEXT, :] = jnp.zeros((3, GRP, 128), F32)
        coef_w[:, GRP + ROWS : CEXT, :] = jnp.zeros((3, GRP, 128), F32)

    for t in range(2):
        cur[t, DEEP : DEEP + ROWS] = field_ref[t]
        coef[t, :, GRP : GRP + ROWS, :] = coef_ref[t]

    greeted = 2 + 3 * has_n.astype(jnp.int32) + 3 * has_s.astype(jnp.int32) + (n_lon - 1) * top.astype(jnp.int32)
    pl.semaphore_wait(barrier, greeted)

    mid_g, low_g, high_g = pl.ds(GRP, ROWS), pl.ds(0, GRP), pl.ds(GRP + ROWS, GRP)
    head, tail = pl.ds(0, GRP), pl.ds(ROWS - GRP, GRP)
    copies = [
        ((pack_e, edge_w.at[pl.ds(2, 6)]), (coef_ref.at[1], coef_w.at[:, mid_g, :])),
        ((pack_w, edge_e.at[pl.ds(2, 6)]), (coef_ref.at[0], coef_e.at[:, mid_g, :])),
        (
            (field_ref.at[:, pl.ds(ROWS - DEEP, DEEP)], cur.at[pl.ds(0, 2), pl.ds(0, DEEP)]),
            (coef_ref.at[:, :, tail, :], coef.at[:, :, low_g, :]),
        ),
        (
            (field_ref.at[:, pl.ds(0, DEEP)], cur.at[pl.ds(0, 2), pl.ds(EXT - DEEP, DEEP)]),
            (coef_ref.at[:, :, head, :], coef.at[:, :, high_g, :]),
        ),
        ((pack_e.at[pl.ds(4, 2)], edge_w.at[pl.ds(0, 2)]), (coef_ref.at[1, :, tail, :], coef_w.at[:, low_g, :])),
        ((pack_w.at[pl.ds(4, 2)], edge_e.at[pl.ds(0, 2)]), (coef_ref.at[0, :, tail, :], coef_e.at[:, low_g, :])),
        ((pack_e.at[pl.ds(0, 2)], edge_w.at[pl.ds(8, 2)]), (coef_ref.at[1, :, head, :], coef_w.at[:, high_g, :])),
        ((pack_w.at[pl.ds(0, 2)], edge_e.at[pl.ds(8, 2)]), (coef_ref.at[0, :, head, :], coef_e.at[:, high_g, :])),
    ]

    def copy_of(w, k):
        source, target = copies[w][k]
        return pltpu.make_async_remote_copy(
            src_ref=source,
            dst_ref=target,
            send_sem=send_sem.at[w, k],
            recv_sem=recv_sem.at[w, k],
            device_id=(ways[w][1], ways[w][2]),
            device_id_type=MESH,
        )

    for w in range(8):
        @pl.when(ways[w][0])
        def _():
            for k in range(2):
                copy_of(w, k).start()

    mine = pl.ds(2 * lon, 2)
    fold_source = field_ref.at[:, pl.ds(ROWS - DEEP, DEEP)]
    coef_source = coef_ref.at[:, :, tail, :]

    def fold_copies(i):
        to = (lat, lax.rem(lon + i, n_lon))
        return [
            pltpu.make_async_remote_copy(
                src_ref=source,
                dst_ref=target.at[mine],
                send_sem=fold_send.at[k, i],
                recv_sem=fold_recv.at[k, i],
                device_id=to,
                device_id_type=MESH,
            )
            for k, (source, target) in enumerate(((fold_source, fold), (coef_source, coef_fold)))
        ]

    def start_fold(i, carry):
        for copy in fold_copies(i):
            copy.start()
        return carry

    def wait_fold(i, carry):
        for copy in fold_copies(i):
            copy.wait()
        return carry

    @pl.when(top)
    def _():
        lax.fori_loop(1, n_lon, start_fold, 0)
        own = [
            pltpu.make_async_copy(fold_source, fold.at[mine], local_sem.at[0]),
            pltpu.make_async_copy(coef_source, coef_fold.at[mine], local_sem.at[1]),
        ]
        for copy in own:
            copy.start()
        for copy in own:
            copy.wait()

    for w in range(8):
        @pl.when(ways[w][0])
        def _():
            for k in range(2):
                copy_of(w, k).wait_send()

        @pl.when(ways[w][3])
        def _():
            for k in range(2):
                copy_of(w, k).wait_recv()

    side = lanes_of((CP, 128)) < 64

    def unpack(i, carry):
        from_e = edge_e[i]
        from_w = edge_w[i]
        for j in range(8):
            x = pltpu.roll(from_e, 128 - 16 * j, 1) if j else from_e
            y = pltpu.roll(from_w, 112 - 16 * j, 1) if j < 7 else from_w
            row = 8 * i + j - (GRP - DEEP)
            nxt[0, row + (GRP - DEEP)] = jnp.where(side, x, y)
        return carry

    lax.fori_loop(0, CEXT // 8, unpack, 0)
    cur[2] = nxt[0, GRP - DEEP : GRP - DEEP + EXT]
    side_c = lanes_of((3, CEXT, 128)) < 64
    coef_e[...] = jnp.where(side_c, coef_e[...], coef_w[...])

    @pl.when(top)
    def _():
        lax.fori_loop(1, n_lon, wait_fold, 0)
        corner = partner_ref[0]
        tile0 = corner // 128
        shift = lax.rem(corner, 128)
        lane = lanes_of((CP, 128))
        index = (shift - lane) & 127
        near = lane <= shift
        places = [lax.rem(tile0 + x - 4 + 2 * n_lon, 2 * n_lon) for x in range(1, 6)]

        def mirrored(load, index, near, side):
            tiles = [jnp.take_along_axis(load(p), index, axis=1) for p in places]
            merged = [jnp.where(near, tiles[x], tiles[x - 1]) for x in range(1, 5)]
            return merged[2], merged[1], jnp.where(side, merged[0], merged[3])

        def ghost(d, carry):
            tiles = mirrored(lambda p: fold[p, DEEP - 1 - d], index, near, side)
            for t in range(3):
                cur[t, EXT - DEEP + d] = tiles[t]
            return carry

        lax.fori_loop(0, DEEP, ghost, 0)
        lane_c = lanes_of((GRP, 128))
        for k in range(3):
            tiles = mirrored(
                lambda p: coef_fold[p, k], (shift - lane_c) & 127, lane_c <= shift, lane_c < 64
            )
            for d in range(GRP):
                for t in range(2):
                    coef[t, k, GRP + ROWS + d : GRP + ROWS + d + 1, :] = tiles[t][GRP - 1 - d : GRP - d]
                coef_e[k, GRP + ROWS + d : GRP + ROWS + d + 1, :] = tiles[2][GRP - 1 - d : GRP - d]

    channel = lax.broadcasted_iota(jnp.int32, (CP, 128), 0)
    level = jnp.where(channel < LEV, channel, jnp.where(channel < 2 * LEV, channel - LEV, 0))
    level = jnp.where(channel < C, level, 2 * LEV).astype(F32)
    scale = jnp.broadcast_to(scale_ref[...], (CP, 128))
    sigma = jnp.broadcast_to(sigma_ref[...], (CP, 128))

    def coef_row(k, row):
        return [
            jnp.broadcast_to(ref[k, pl.ds(row, 1), :], (CP, 128))
            for ref in (coef.at[0], coef.at[1], coef_e)
        ]

    def weigh(r, carry):
        g = r + (GRP - DEEP)
        wet_here = [(level < b).astype(F32) for b in coef_row(0, g)]
        wet_north = [(level < b).astype(F32) for b in coef_row(0, g + 1)]
        wet_south = [(level < b).astype(F32) for b in coef_row(0, g - 1)]
        k0 = coef_row(1, g)
        k1 = coef_row(2, g)
        k1_north = coef_row(2, g + 1)
        k1_south = coef_row(2, g - 1)
        k0_east, k0_west = east_of(k0), west_of(k0)
        wet_east, wet_west = east_of(wet_here), west_of(wet_here)
        for t in range(3):
            here = scale * wet_here[t]
            e = here * (0.5 * (k0[t] + k0_east[t])) * wet_east[t]
            w = here * (0.5 * (k0[t] + k0_west[t])) * wet_west[t]
            m = here * (0.5 * (k1[t] + k1_north[t])) * wet_north[t]
            s = here * (0.5 * (k1[t] + k1_south[t])) * wet_south[t]
            over = 1.0 / (1.0 + e + w + m + s)
            inv[t, r] = over
            w_e[t, r] = e * over
            w_w[t, r] = w * over
            w_n[t, r] = m * over
            w_s[t, r] = s * over
            start = jnp.where(wet_here[t] > 0.0, cur[t, r] * sigma, 0.0)
            cur[t, r] = start
            rhs[t, r] = start * over
        return carry

    lax.fori_loop(0, EXT, weigh, 0)

    def sweep(source, target, r):
        here = [source[t, r] for t in range(3)]
        to_east, to_west = east_of(here), west_of(here)
        for t in range(3):
            target[t, r] = (
                rhs[t, r]
                + w_e[t, r] * to_east[t]
                + w_w[t, r] * to_west[t]
                + w_n[t, r] * source[t, r + 1]
                + w_s[t, r] * source[t, r - 1]
            )

    source, target = cur, nxt
    for s in range(1, DEEP + 1):
        if s == DEEP // 2 + 1:
            def renew(r, carry, source=source):
                for t in range(3):
                    rhs[t, r] = source[t, r] * inv[t, r]
                return carry

            lax.fori_loop(s, EXT - s, renew, 0)

        def rows(r, carry, source=source, target=target):
            sweep(source, target, r)
            return carry

        lax.fori_loop(s, EXT - s, rows, 0, unroll=2)
        source, target = target, source

    def finish(r, carry):
        for t in range(2):
            out_ref[t, r] = source[t, r + DEEP] * sigma
        return carry

    lax.fori_loop(0, ROWS, finish, 0)


def diffuse(n_lat, n_lon, partner, field, coef, scale, sigma):
    vmem = pl.BlockSpec(memory_space=pltpu.VMEM)
    state = pltpu.VMEM((3, EXT, CP, 128), F32)
    state_wide = pltpu.VMEM((3, CEXT, CP, 128), F32)
    return pl.pallas_call(
        functools.partial(diffuse_kernel, n_lat, n_lon),
        out_shape=jax.ShapeDtypeStruct((2, ROWS, CP, 128), F32),
        in_specs=[pl.BlockSpec(memory_space=pltpu.SMEM), vmem, vmem, vmem, vmem],
        out_specs=vmem,
        scratch_shapes=[
            state,
            state_wide,
            state,
            state,
            state,
            state,
            state,
            state,
            pltpu.VMEM((ROWS // 8, CP, 128), F32),
            pltpu.VMEM((ROWS // 8, CP, 128), F32),
            pltpu.VMEM((CEXT // 8, CP, 128), F32),
            pltpu.VMEM((CEXT // 8, CP, 128), F32),
            pltpu.VMEM((2, 3, CEXT, 128), F32),
            pltpu.VMEM((3, CEXT, 128), F32),
            pltpu.VMEM((3, CEXT, 128), F32),
            pltpu.VMEM((2 * n_lon, DEEP, CP, 128), F32),
            pltpu.VMEM((2 * n_lon, 3, GRP, 128), F32),
            pltpu.SemaphoreType.DMA((8, 2)),
            pltpu.SemaphoreType.DMA((8, 2)),
            pltpu.SemaphoreType.DMA((2, n_lon)),
            pltpu.SemaphoreType.DMA((2, n_lon)),
            pltpu.SemaphoreType.DMA((2,)),
        ],
        compiler_params=pltpu.CompilerParams(
            collective_id=1, has_side_effects=True, vmem_limit_bytes=VMEM_LIMIT
        ),
        name="diffuse",
    )(partner, field, coef, scale, sigma)


def gather_kernel(n, n_lon, size, slot_ref, state_ref, out_ref, pieces, onehot, fits, send_sem, recv_sem, local_sem):
    me = lax.axis_index("lat") * n_lon + lax.axis_index("lon")
    barrier = pltpu.get_barrier_semaphore()

    def greet(i, carry):
        pl.semaphore_signal(barrier, inc=1, device_id=place_of(lax.rem(me + i, n), n_lon), device_id_type=MESH)
        return carry

    lax.fori_loop(1, n, greet, 0)
    for b in range(0, BAND, 2):
        for half in range(2):
            for t in range(2):
                rows = jnp.concatenate(
                    [state_ref[t, 2 * b + half], state_ref[t, 2 * b + 2 + half]], axis=0
                )
                high = rows.astype(BF16)
                low = (rows - high.astype(F32)).astype(BF16)
                first = half * COLS + t * 128
                pieces[b * CP : (b + 2) * CP, first : first + 128] = high
                pieces[b * CP : (b + 2) * CP, PLACES + first : PLACES + first + 128] = low
    pl.semaphore_wait(barrier, n - 1)

    def chunk(g, carry):
        for j in range(size):
            band, halves = split(slot_ref[pl.ds(g * size + j, 1), :])
            store_onehot(onehot, halves, slice(j * 128, (j + 1) * 128))
        picked = jnp.dot(pieces[:, :PLACES], onehot[...], preferred_element_type=F32) + jnp.dot(
            pieces[:, PLACES:], onehot[...], preferred_element_type=F32
        )
        for j in range(size):
            band, halves = split(slot_ref[pl.ds(g * size + j, 1), :])
            band = jnp.broadcast_to(band, (CP, 128))
            fit = jnp.zeros((CP, 128), F32)
            for b in range(BAND):
                fit += jnp.where(band == b, picked[b * CP : (b + 1) * CP, j * 128 : (j + 1) * 128], 0.0)
            fits[g * size + j] = fit
        for j in range(size):
            i = g * size + j
            to = lax.rem(me - i + n, n)

            @pl.when(i > 0)
            def _():
                pltpu.make_async_remote_copy(
                    src_ref=fits.at[i, 0:C, :],
                    dst_ref=out_ref.at[:, me, :],
                    send_sem=send_sem,
                    recv_sem=recv_sem,
                    device_id=place_of(to, n_lon),
                    device_id_type=MESH,
                ).start()

            @pl.when(i == 0)
            def _():
                pltpu.make_async_copy(fits.at[0, 0:C, :], out_ref.at[:, me, :], local_sem).start()

        return carry

    lax.fori_loop(0, n // size, chunk, 0)
    pltpu.make_async_copy(fits.at[0, 0:C, :], out_ref.at[:, me, :], local_sem).wait()
    sent = fits.at[1:n, 0:C, :]
    pltpu.make_async_copy(sent, sent, send_sem).wait()
    pltpu.make_async_copy(sent, sent, recv_sem).wait()


def gather(n, n_lon, slot, state):
    size = min(4, n // 4)
    vmem = pl.BlockSpec(memory_space=pltpu.VMEM)
    return pl.pallas_call(
        functools.partial(gather_kernel, n, n_lon, size),
        out_shape=jax.ShapeDtypeStruct((C, n, 128), F32),
        in_specs=[vmem, vmem],
        out_specs=vmem,
        scratch_shapes=[
            pltpu.VMEM((BAND * CP, 2 * PLACES), BF16),
            pltpu.VMEM((PLACES, size * 128), BF16),
            pltpu.VMEM((n, CP, 128), F32),
            pltpu.SemaphoreType.DMA,
            pltpu.SemaphoreType.DMA,
            pltpu.SemaphoreType.DMA,
        ],
        compiler_params=pltpu.CompilerParams(
            collective_id=2, has_side_effects=True, vmem_limit_bytes=VMEM_LIMIT
        ),
        name="gather",
    )(slot, state)


def per_device(
    n_lat, n_lon, obs_value, obs_cell, obs_count, bottom_level, diffusivity, partner, length_scale, sigma
):
    n = n_lat * n_lon
    slots = lax.broadcasted_iota(jnp.int32, (n, 128), 1)
    cell = jnp.where(slots < obs_count[0][:, None], obs_cell[0], -1).astype(F32)
    coef = jnp.concatenate([bottom_level.astype(F32)[None], diffusivity], axis=0)
    coef = coef.reshape(3, ROWS, 2, 128).transpose(2, 0, 1, 3)
    column = lambda x: jnp.pad(x, (0, CP - C))[:, None]
    field, slot = scatter(n, n_lon, obs_value[0], cell)
    state = diffuse(n_lat, n_lon, partner, field, coef, column(length_scale), column(sigma))
    fit = gather(n, n_lon, slot, state)
    diffused = state[:, :, :C, :].transpose(2, 1, 0, 3).reshape(C, ROWS, COLS)
    return fit[None], diffused


def solution(mesh):
    n_lat, n_lon = mesh.shape["lat"], mesh.shape["lon"]
    return jax.shard_map(
        functools.partial(per_device, n_lat, n_lon),
        mesh=mesh,
        in_specs=(
            P(("lat", "lon"), None, None, None),
            P(("lat", "lon"), None, None),
            P(("lat", "lon"), None),
            P("lat", "lon"),
            P(None, "lat", "lon"),
            P("lon"),
            P(),
            P(),
        ),
        out_specs=(P(("lat", "lon"), None, None, None), P(None, "lat", "lon")),
        check_vma=False,
    )
```

```python
import functools

import jax
import jax.numpy as jnp
from jax import lax
from jax.experimental import pallas as pl
from jax.experimental.pallas import tpu as pltpu
from jax.sharding import PartitionSpec as P

LEV = 10
C = 21
CP = 24
ROWS = 48
COLS = 256
BAND = ROWS // 2
PLACES = 2 * COLS
DEEP = 12
EXT = ROWS + 2 * DEEP
GRP = 16
CEXT = ROWS + 2 * GRP
F32 = jnp.float32
BF16 = jnp.bfloat16
MESH = pl.DeviceIdType.MESH
VMEM_LIMIT = 60 * 2**20


def place_of(linear, n_lon):
    return (linear // n_lon, lax.rem(linear, n_lon))


def split(cell):
    cell = cell.astype(jnp.int32)
    place = cell & (PLACES - 1)
    low = place & 255
    half = place >> 8
    return cell >> 9, [jnp.where(half == h, low, 512).astype(F32) for h in range(2)]


def store_onehot(onehot, halves, lanes):
    one = jnp.ones((16, 128), BF16)
    zero = jnp.zeros((16, 128), BF16)
    steps = lax.broadcasted_iota(jnp.int32, (16, 128), 0).astype(F32).astype(BF16)
    for h in range(2):
        row = jnp.broadcast_to(halves[h], (16, 128)).astype(BF16)
        for t in range(16):
            first = h * 256 + t * 16
            onehot[first : first + 16, lanes] = jnp.where(row == steps + BF16(16 * t), one, zero)


def build_chunk(arrived, chunk, size, lhs, onehot):
    for j in range(size):
        value = arrived[chunk * size + j]
        band, halves = split(value[C : C + 1, :])
        lanes = slice(j * 128, (j + 1) * 128)
        high = value.astype(BF16)
        pieces = jnp.concatenate([value, value - high.astype(F32)], axis=0).astype(BF16)
        band = jnp.broadcast_to(band.astype(F32), (16, 128)).astype(BF16)
        zero = jnp.zeros((2 * CP, 128), BF16)
        for b in range(BAND):
            mask = jnp.concatenate([band == BF16(b)] * 3, axis=0)
            lhs[b * 2 * CP : (b + 1) * 2 * CP, lanes] = jnp.where(mask, pieces, zero)
        store_onehot(onehot, halves, lanes)


def lanes_of(shape):
    return lax.broadcasted_iota(jnp.int32, shape, len(shape) - 1)


def east_of(tiles):
    turned = [pltpu.roll(x, 127, x.ndim - 1) for x in tiles]
    last = lanes_of(tiles[0].shape) == 127
    return [jnp.where(last, turned[(t + 1) % 3], turned[t]) for t in range(3)]


def west_of(tiles):
    turned = [pltpu.roll(x, 1, x.ndim - 1) for x in tiles]
    first = lanes_of(tiles[0].shape) == 0
    return [jnp.where(first, turned[(t + 2) % 3], turned[t]) for t in range(3)]


def sweep(source, target, rhs, weights, first, stop, unroll):
    w_e, w_w, w_n, w_s = weights
    unroll = min(unroll, stop - first)

    def block(i, carry):
        start = jnp.minimum(first + i * unroll, stop - unroll)
        for c in range(0, CP, 8):
            part = pl.ds(c, 8)
            below = [source[t, start - 1, part] for t in range(3)]
            here = [source[t, start, part] for t in range(3)]
            for k in range(unroll):
                r = start + k
                above = [source[t, r + 1, part] for t in range(3)]
                to_east, to_west = east_of(here), west_of(here)
                for t in range(3):
                    target[t, r, part] = (
                        (rhs[t, r, part] + w_n[t, r, part] * above[t])
                        + (w_s[t, r, part] * below[t] + w_e[t, r, part] * to_east[t])
                        + w_w[t, r, part] * to_west[t]
                    )
                below, here = here, above
        return carry

    lax.fori_loop(0, -(-(stop - first) // unroll), block, 0)


def kernel(
    n_lat, n_lon, size, back, partner_ref, value_ref, cell_ref, coef_ref, scale_ref, sigma_ref, out_ref, state_ref,
    outgoing, arrived, lhs0, onehot0, lhs1, onehot1, total, field, fits, pieces,
    cur, nxt, rhs, inv, w_e, w_w, w_n, w_s, pack_e, pack_w, edge_e, edge_w,
    coef, coef_e, coef_w, fold, coef_fold,
    local_sem, obs_send, obs_recv, way_send, way_recv, fold_send, fold_recv, back_send, back_recv,
):
    n = n_lat * n_lon
    lat = lax.axis_index("lat")
    lon = lax.axis_index("lon")
    me = lat * n_lon + lon
    top = lat == n_lat - 1
    load = pltpu.make_async_copy(value_ref, outgoing.at[0:C], local_sem.at[0])
    load.start()
    barrier = pltpu.get_barrier_semaphore()

    def greet(i, carry):
        pl.semaphore_signal(barrier, inc=1, device_id=place_of(lax.rem(me + i, n), n_lon), device_id_type=MESH)
        return carry

    @pl.when(lat == 0)
    def _():
        cur[0:2, 0:DEEP] = jnp.zeros((2, DEEP, CP, 128), F32)
        edge_e[0:2] = jnp.zeros((2, CP, 128), F32)
        edge_w[0:2] = jnp.zeros((2, CP, 128), F32)
        coef[:, :, 0:GRP, :] = jnp.zeros((2, 3, GRP, 128), F32)
        coef_e[:, 0:GRP, :] = jnp.zeros((3, GRP, 128), F32)
        coef_w[:, 0:GRP, :] = jnp.zeros((3, GRP, 128), F32)

    @pl.when(top)
    def _():
        edge_e[8:10] = jnp.zeros((2, CP, 128), F32)
        edge_w[8:10] = jnp.zeros((2, CP, 128), F32)
        coef_e[:, GRP + ROWS : CEXT, :] = jnp.zeros((3, GRP, 128), F32)
        coef_w[:, GRP + ROWS : CEXT, :] = jnp.zeros((3, GRP, 128), F32)

    lax.fori_loop(1, n, greet, 0)
    outgoing[C] = cell_ref[...]
    total[...] = jnp.zeros_like(total)
    for t in range(2):
        coef[t, :, GRP : GRP + ROWS, :] = coef_ref[t]
    load.wait()
    pl.semaphore_wait(barrier, n - 1)

    east = lax.rem(lon + 1, n_lon)
    west = lax.rem(lon + n_lon - 1, n_lon)
    has_n = lat < n_lat - 1
    has_s = lat > 0
    everywhere = lat >= 0
    north = jnp.minimum(lat + 1, n_lat - 1)
    south = jnp.maximum(lat - 1, 0)
    ways = [
        (everywhere, lat, east, everywhere),
        (everywhere, lat, west, everywhere),
        (has_n, north, lon, has_s),
        (has_n, north, east, has_s),
        (has_n, north, west, has_s),
        (has_s, south, lon, has_n),
        (has_s, south, east, has_n),
        (has_s, south, west, has_n),
    ]
    mid_g, low_g, high_g = pl.ds(GRP, ROWS), pl.ds(0, GRP), pl.ds(GRP + ROWS, GRP)
    head, tail = pl.ds(0, GRP), pl.ds(ROWS - GRP, GRP)
    copies = [
        ((pack_e, edge_w.at[pl.ds(2, 6)]), (coef_ref.at[1], coef_w.at[:, mid_g, :])),
        ((pack_w, edge_e.at[pl.ds(2, 6)]), (coef_ref.at[0], coef_e.at[:, mid_g, :])),
        (
            (field.at[:, pl.ds(ROWS - DEEP, DEEP)], cur.at[pl.ds(0, 2), pl.ds(0, DEEP)]),
            (coef_ref.at[:, :, tail, :], coef.at[:, :, low_g, :]),
        ),
        ((pack_e.at[pl.ds(4, 2)], edge_w.at[pl.ds(0, 2)]), (coef_ref.at[1, :, tail, :], coef_w.at[:, low_g, :])),
        ((pack_w.at[pl.ds(4, 2)], edge_e.at[pl.ds(0, 2)]), (coef_ref.at[0, :, tail, :], coef_e.at[:, low_g, :])),
        (
            (field.at[:, pl.ds(0, DEEP)], cur.at[pl.ds(0, 2), pl.ds(EXT - DEEP, DEEP)]),
            (coef_ref.at[:, :, head, :], coef.at[:, :, high_g, :]),
        ),
        ((pack_e.at[pl.ds(0, 2)], edge_w.at[pl.ds(8, 2)]), (coef_ref.at[1, :, head, :], coef_w.at[:, high_g, :])),
        ((pack_w.at[pl.ds(0, 2)], edge_e.at[pl.ds(8, 2)]), (coef_ref.at[0, :, head, :], coef_e.at[:, high_g, :])),
    ]

    def copy_of(w, k):
        source, target = copies[w][k]
        return pltpu.make_async_remote_copy(
            src_ref=source,
            dst_ref=target,
            send_sem=way_send.at[w, k],
            recv_sem=way_recv.at[w, k],
            device_id=(ways[w][1], ways[w][2]),
            device_id_type=MESH,
        )

    def start_ways(k):
        for w in range(8):
            @pl.when(ways[w][0])
            def _():
                copy_of(w, k).start()

    def wait_ways(k, which):
        for w in which:
            @pl.when(ways[w][3])
            def _():
                copy_of(w, k).wait_recv()

    def drain_ways(k):
        for w in range(8):
            @pl.when(ways[w][0])
            def _():
                copy_of(w, k).wait_send()

    mine = pl.ds(2 * lon, 2)
    folds = [
        (field.at[:, pl.ds(ROWS - DEEP, DEEP)], fold),
        (coef_ref.at[:, :, tail, :], coef_fold),
    ]

    def fold_copy(k, i):
        source, target = folds[k]
        return pltpu.make_async_remote_copy(
            src_ref=source,
            dst_ref=target.at[mine],
            send_sem=fold_send.at[k, i],
            recv_sem=fold_recv.at[k, i],
            device_id=(lat, lax.rem(lon + i, n_lon)),
            device_id_type=MESH,
        )

    def start_fold(k):
        def one(i, carry):
            fold_copy(k, i).start()
            return carry

        lax.fori_loop(1, n_lon, one, 0)
        own = pltpu.make_async_copy(folds[k][0], folds[k][1].at[mine], local_sem.at[1])
        own.start()
        own.wait()

    def wait_fold(k):
        def one(i, carry):
            fold_copy(k, i).wait()
            return carry

        lax.fori_loop(1, n_lon, one, 0)

    corner = partner_ref[0]
    tile0 = corner // 128
    shift = lax.rem(corner, 128)
    places = [lax.rem(tile0 + x - 4 + 2 * n_lon, 2 * n_lon) for x in range(1, 6)]

    def mirrored(load, rows):
        lane = lanes_of((rows, 128))
        index = (shift - lane) & 127
        near = lane <= shift
        tiles = [jnp.take_along_axis(load(p), index, axis=1) for p in places]
        merged = [jnp.where(near, tiles[x], tiles[x - 1]) for x in range(1, 5)]
        return merged[2], merged[1], jnp.where(lane < 64, merged[0], merged[3])

    start_ways(1)

    @pl.when(top)
    def _():
        start_fold(1)

    def send(i, carry):
        owner = lax.rem(me + i, n)
        pltpu.make_async_remote_copy(
            src_ref=outgoing.at[:, owner, :],
            dst_ref=arrived.at[i, 0 : C + 1, :],
            send_sem=obs_send,
            recv_sem=obs_recv.at[i // size],
            device_id=place_of(owner, n_lon),
            device_id_type=MESH,
        ).start()
        return carry

    own_obs = pltpu.make_async_copy(outgoing.at[:, me, :], arrived.at[0, 0 : C + 1, :], local_sem.at[0])
    own_obs.start()
    lax.fori_loop(1, n, send, 0)

    wait_ways(1, range(8))
    side_c = lanes_of((3, CEXT, 128)) < 64
    coef_e[...] = jnp.where(side_c, coef_e[...], coef_w[...])

    @pl.when(top)
    def _():
        wait_fold(1)
        for k in range(3):
            tiles = mirrored(lambda p: coef_fold[p, k], GRP)
            for d in range(GRP):
                row = GRP + ROWS + d
                for t in range(2):
                    coef[t, k, row : row + 1, :] = tiles[t][GRP - 1 - d : GRP - d]
                coef_e[k, row : row + 1, :] = tiles[2][GRP - 1 - d : GRP - d]

    channel = lax.broadcasted_iota(jnp.int32, (CP, 128), 0)
    level = jnp.where(channel < LEV, channel, jnp.where(channel < 2 * LEV, channel - LEV, 0))
    level = jnp.where(channel < C, level, 2 * LEV).astype(F32)
    scale = jnp.broadcast_to(scale_ref[...], (CP, 128))
    sigma = jnp.broadcast_to(sigma_ref[...], (CP, 128))

    def coef_row(k, row):
        return [
            jnp.broadcast_to(ref[k, pl.ds(row, 1), :], (CP, 128))
            for ref in (coef.at[0], coef.at[1], coef_e)
        ]

    def weigh(r, carry):
        g = r + (GRP - DEEP)
        deep, deep_n, deep_s = coef_row(0, g), coef_row(0, g + 1), coef_row(0, g - 1)
        k0 = coef_row(1, g)
        k1, k1_n, k1_s = coef_row(2, g), coef_row(2, g + 1), coef_row(2, g - 1)
        k0_east, k0_west = east_of(k0), west_of(k0)
        deep_east, deep_west = east_of(deep), west_of(deep)
        for t in range(3):
            def face(k, deep_there):
                both = level < jnp.minimum(deep[t], deep_there)
                return jnp.where(both, scale * (0.5 * k), 0.0)

            e = face(k0[t] + k0_east[t], deep_east[t])
            w = face(k0[t] + k0_west[t], deep_west[t])
            m = face(k1[t] + k1_n[t], deep_n[t])
            s = face(k1[t] + k1_s[t], deep_s[t])
            over = 1.0 / (1.0 + e + w + m + s)
            inv[t, r] = over
            w_e[t, r] = e * over
            w_w[t, r] = w * over
            w_n[t, r] = m * over
            w_s[t, r] = s * over
        return carry

    lax.fori_loop(0, EXT, weigh, 0)
    drain_ways(1)

    def arrive(chunk, first):
        window = arrived.at[pl.ds(chunk * size + first, size - first), 0 : C + 1, :]
        pltpu.make_async_copy(window, window, obs_recv.at[chunk]).wait()

    chunks = n // size
    dims = (((1,), (1,)), ((), ()))
    own_obs.wait()
    arrive(0, 1)
    build_chunk(arrived, 0, size, lhs0, onehot0)

    def pair(i, carry):
        arrive(2 * i + 1, 0)
        build_chunk(arrived, 2 * i + 1, size, lhs1, onehot1)
        total[...] += lax.dot_general(lhs0[...], onehot0[...], dims, preferred_element_type=F32)
        more = 2 * i + 2

        @pl.when(more < chunks)
        def _():
            arrive(more, 0)

        build_chunk(arrived, jnp.minimum(more, chunks - 1), size, lhs0, onehot0)
        total[...] += lax.dot_general(lhs1[...], onehot1[...], dims, preferred_element_type=F32)
        return carry

    lax.fori_loop(0, chunks // 2, pair, 0)
    for b in range(BAND):
        first = b * 2 * CP
        band = total[first : first + CP, :] + total[first + CP : first + 2 * CP, :]
        for t in range(4):
            field[t % 2, 2 * b + t // 2] = band[:, t * 128 : (t + 1) * 128]

    lane16 = lanes_of((CP, 128)) >> 4
    for i in range(ROWS // 8):
        first = jnp.zeros((CP, 128), F32)
        last = jnp.zeros((CP, 128), F32)
        for j in range(8):
            x = field[0, 8 * i + j]
            y = field[1, 8 * i + j]
            first = jnp.where(lane16 == j, pltpu.roll(x, 16 * j, 1) if j else x, first)
            last = jnp.where(lane16 == j, pltpu.roll(y, 16 * j + 16, 1) if j < 7 else y, last)
        pack_w[i] = first
        pack_e[i] = last

    start_ways(0)

    @pl.when(top)
    def _():
        start_fold(0)

    def begin(r, tiles):
        deep = coef_row(0, r + (GRP - DEEP))
        for t in range(3):
            start = jnp.where(level < deep[t], tiles[t] * sigma, 0.0)
            cur[t, r] = start
            rhs[t, r] = start * inv[t, r]

    side = lanes_of((CP, 128)) < 64

    def unpack(i):
        from_e = edge_e[i]
        from_w = edge_w[i]
        for j in range(8):
            x = pltpu.roll(from_e, 128 - 16 * j, 1) if j else from_e
            y = pltpu.roll(from_w, 112 - 16 * j, 1) if j < 7 else from_w
            row = 8 * i + j - (GRP - DEEP)
            if 0 <= row < EXT:
                cur[2, row] = jnp.where(side, x, y)

    def begin_own(r, carry):
        begin(r, [field[0, r - DEEP], field[1, r - DEEP], cur[2, r]])
        return carry

    def begin_ghost(r, carry):
        begin(r, [cur[t, r] for t in range(3)])
        return carry

    wait_ways(0, range(0, 5))
    for i in range(0, 8):
        unpack(i)
    lax.fori_loop(0, DEEP, begin_ghost, 0)
    lax.fori_loop(DEEP, DEEP + ROWS, begin_own, 0, unroll=2)

    weights = (w_e, w_w, w_n, w_s)
    buffers = [cur, nxt]

    def renew(first, stop):
        def one(r, carry):
            for t in range(3):
                rhs[t, r] = cur[t, r] * inv[t, r]
            return carry

        lax.fori_loop(first, stop, one, 0, unroll=2)

    limit = DEEP + ROWS
    for s in range(1, DEEP + 1):
        if s == DEEP // 2 + 1:
            renew(s, limit - s)
        sweep(buffers[(s - 1) % 2], buffers[s % 2], rhs, weights, s, limit - s, 12)

    wait_ways(0, range(5, 8))
    for i in range(8, 10):
        unpack(i)

    @pl.when(top)
    def _():
        wait_fold(0)

        def ghost(d, carry):
            tiles = mirrored(lambda p: fold[p, DEEP - 1 - d], CP)
            for t in range(3):
                cur[t, limit + d] = tiles[t]
            return carry

        lax.fori_loop(0, DEEP, ghost, 0)

    lax.fori_loop(limit, EXT, begin_ghost, 0)
    for s in range(1, DEEP + 1):
        if s == DEEP // 2 + 1:
            renew(limit - s, EXT - s)
        sweep(buffers[(s - 1) % 2], buffers[s % 2], rhs, weights, limit - s, EXT - s, 12)

    for b in range(0, BAND, 2):
        for half in range(2):
            for t in range(2):
                rows = []
                for row in (2 * b + half, 2 * b + 2 + half):
                    value = cur[t, row + DEEP] * sigma
                    state_ref[t, row] = value
                    rows.append(value)
                rows = jnp.concatenate(rows, axis=0)
                high = rows.astype(BF16)
                low = (rows - high.astype(F32)).astype(BF16)
                first = half * COLS + t * 128
                pieces[b * CP : (b + 2) * CP, first : first + 128] = high
                pieces[b * CP : (b + 2) * CP, PLACES + first : PLACES + first + 128] = low

    def chunk(g, carry):
        bands = []
        for j in range(back):
            band, halves = split(arrived[g * back + j, C : C + 1, :])
            bands.append(band)
            store_onehot(onehot0, halves, slice(j * 128, (j + 1) * 128))
        hot = onehot0[:, : back * 128]
        picked = jnp.dot(pieces[:, :PLACES], hot, preferred_element_type=F32) + jnp.dot(
            pieces[:, PLACES:], hot, preferred_element_type=F32
        )
        for j in range(back):
            band = jnp.broadcast_to(bands[j], (CP, 128))
            fit = jnp.zeros((CP, 128), F32)
            for b in range(BAND):
                fit += jnp.where(band == b, picked[b * CP : (b + 1) * CP, j * 128 : (j + 1) * 128], 0.0)
            fits[g * back + j] = fit
        for j in range(back):
            i = g * back + j
            to = lax.rem(me - i + n, n)

            @pl.when(i > 0)
            def _():
                pltpu.make_async_remote_copy(
                    src_ref=fits.at[i, 0:C, :],
                    dst_ref=out_ref.at[:, me, :],
                    send_sem=back_send,
                    recv_sem=back_recv,
                    device_id=place_of(to, n_lon),
                    device_id_type=MESH,
                ).start()

        return carry

    lax.fori_loop(0, n // back, chunk, 0)
    own_fit = pltpu.make_async_copy(fits.at[0, 0:C, :], out_ref.at[:, me, :], local_sem.at[0])
    own_fit.start()
    own_fit.wait()
    drain_ways(0)
    sent = arrived.at[1:n, 0 : C + 1, :]
    pltpu.make_async_copy(sent, sent, obs_send).wait()
    sent = fits.at[1:n, 0:C, :]
    pltpu.make_async_copy(sent, sent, back_send).wait()
    pltpu.make_async_copy(sent, sent, back_recv).wait()


def run(n_lat, n_lon, partner, value, cell, coef, scale, sigma):
    n = n_lat * n_lon
    size = min(8, n // 4)
    back = min(4, n // 4)
    vmem = pl.BlockSpec(memory_space=pltpu.VMEM)
    buffers = [
        pltpu.VMEM((BAND * 2 * CP, size * 128), BF16),
        pltpu.VMEM((PLACES, size * 128), BF16),
    ]
    state = pltpu.VMEM((3, EXT, CP, 128), F32)
    return pl.pallas_call(
        functools.partial(kernel, n_lat, n_lon, size, back),
        out_shape=(
            jax.ShapeDtypeStruct((C, n, 128), F32),
            jax.ShapeDtypeStruct((2, ROWS, CP, 128), F32),
        ),
        in_specs=[
            pl.BlockSpec(memory_space=pltpu.SMEM),
            pl.BlockSpec(memory_space=pl.ANY),
            vmem,
            vmem,
            vmem,
            vmem,
        ],
        out_specs=(vmem, vmem),
        scratch_shapes=[
            pltpu.VMEM((C + 1, n, 128), F32),
            pltpu.VMEM((n, CP, 128), F32),
            *buffers,
            *buffers,
            pltpu.VMEM((BAND * 2 * CP, PLACES), F32),
            pltpu.VMEM((2, ROWS, CP, 128), F32),
            pltpu.VMEM((n, CP, 128), F32),
            pltpu.VMEM((BAND * CP, 2 * PLACES), BF16),
            *[state] * 8,
            pltpu.VMEM((ROWS // 8, CP, 128), F32),
            pltpu.VMEM((ROWS // 8, CP, 128), F32),
            pltpu.VMEM((CEXT // 8, CP, 128), F32),
            pltpu.VMEM((CEXT // 8, CP, 128), F32),
            pltpu.VMEM((2, 3, CEXT, 128), F32),
            pltpu.VMEM((3, CEXT, 128), F32),
            pltpu.VMEM((3, CEXT, 128), F32),
            pltpu.VMEM((2 * n_lon, DEEP, CP, 128), F32),
            pltpu.VMEM((2 * n_lon, 3, GRP, 128), F32),
            pltpu.SemaphoreType.DMA((2,)),
            pltpu.SemaphoreType.DMA,
            pltpu.SemaphoreType.DMA((n // size,)),
            pltpu.SemaphoreType.DMA((8, 2)),
            pltpu.SemaphoreType.DMA((8, 2)),
            pltpu.SemaphoreType.DMA((2, n_lon)),
            pltpu.SemaphoreType.DMA((2, n_lon)),
            pltpu.SemaphoreType.DMA,
            pltpu.SemaphoreType.DMA,
        ],
        compiler_params=pltpu.CompilerParams(
            collective_id=0, has_side_effects=True, vmem_limit_bytes=VMEM_LIMIT
        ),
        name="covariance",
    )(partner, value, cell, coef, scale, sigma)


def per_device(
    n_lat, n_lon, obs_value, obs_cell, obs_count, bottom_level, diffusivity, partner, length_scale, sigma
):
    n = n_lat * n_lon
    slots = lax.broadcasted_iota(jnp.int32, (n, 128), 1)
    cell = jnp.where(slots < obs_count[0][:, None], obs_cell[0], -1).astype(F32)
    coef = jnp.concatenate([bottom_level.astype(F32)[None], diffusivity], axis=0)
    coef = coef.reshape(3, ROWS, 2, 128).transpose(2, 0, 1, 3)
    column = lambda x: jnp.pad(x, (0, CP - C))[:, None]
    fit, state = run(
        n_lat, n_lon, partner, obs_value[0], cell, coef, column(length_scale), column(sigma)
    )
    diffused = state[:, :, :C, :].transpose(2, 1, 0, 3).reshape(C, ROWS, COLS)
    return fit[None], diffused


def solution(mesh):
    n_lat, n_lon = mesh.shape["lat"], mesh.shape["lon"]
    return jax.shard_map(
        functools.partial(per_device, n_lat, n_lon),
        mesh=mesh,
        in_specs=(
            P(("lat", "lon"), None, None, None),
            P(("lat", "lon"), None, None),
            P(("lat", "lon"), None),
            P("lat", "lon"),
            P(None, "lat", "lon"),
            P("lon"),
            P(),
            P(),
        ),
        out_specs=(P(("lat", "lon"), None, None, None), P(None, "lat", "lon")),
        check_vma=False,
    )
```

```python
import functools

import jax
import jax.numpy as jnp
from jax import lax
from jax.experimental import pallas as pl
from jax.experimental.pallas import tpu as pltpu
from jax.sharding import PartitionSpec as P

LEV = 10
SWEEPS = 6
C = 21
CP = 24
ROWS = 48
COLS = 256
BAND = ROWS // 2
PLACES = 2 * COLS
DEEP = 12
EXT = ROWS + 2 * DEEP
GRP = 16
CEXT = ROWS + 2 * GRP
F32 = jnp.float32
BF16 = jnp.bfloat16
MESH = pl.DeviceIdType.MESH
VMEM_LIMIT = 60 * 2**20


def place_of(linear, n_lon):
    return (linear // n_lon, lax.rem(linear, n_lon))


def split(cell):
    cell = cell.astype(jnp.int32)
    place = cell & (PLACES - 1)
    low = place & 255
    half = place >> 8
    return cell >> 9, [jnp.where(half == h, low, 512).astype(F32) for h in range(2)]


def store_onehot(onehot, halves, lanes):
    one = jnp.ones((16, 128), BF16)
    zero = jnp.zeros((16, 128), BF16)
    steps = lax.broadcasted_iota(jnp.int32, (16, 128), 0).astype(F32).astype(BF16)
    for h in range(2):
        row = jnp.broadcast_to(halves[h], (16, 128)).astype(BF16)
        for t in range(16):
            first = h * 256 + t * 16
            onehot[first : first + 16, lanes] = jnp.where(row == steps + BF16(16 * t), one, zero)


def build_chunk(arrived, chunk, size, lhs, onehot):
    for j in range(size):
        value = arrived[chunk * size + j]
        band, halves = split(value[C : C + 1, :])
        lanes = slice(j * 128, (j + 1) * 128)
        high = value.astype(BF16)
        pieces = jnp.concatenate([value, value - high.astype(F32)], axis=0).astype(BF16)
        band = jnp.broadcast_to(band.astype(F32), (16, 128)).astype(BF16)
        zero = jnp.zeros((2 * CP, 128), BF16)
        for b in range(BAND):
            mask = jnp.concatenate([band == BF16(b)] * 3, axis=0)
            lhs[b * 2 * CP : (b + 1) * 2 * CP, lanes] = jnp.where(mask, pieces, zero)
        store_onehot(onehot, halves, lanes)


def lanes_of(shape):
    return lax.broadcasted_iota(jnp.int32, shape, len(shape) - 1)


def east_of(tiles):
    turned = [pltpu.roll(x, 127, x.ndim - 1) for x in tiles]
    last = lanes_of(tiles[0].shape) == 127
    return [jnp.where(last, turned[(t + 1) % 3], turned[t]) for t in range(3)]


def west_of(tiles):
    turned = [pltpu.roll(x, 1, x.ndim - 1) for x in tiles]
    first = lanes_of(tiles[0].shape) == 0
    return [jnp.where(first, turned[(t + 2) % 3], turned[t]) for t in range(3)]


def sweep(source, target, rhs, weights, first, stop, unroll):
    w_e, w_w, w_n, w_s = weights

    def block(i, carry):
        start = jnp.minimum(first + i * unroll, stop - unroll)
        for c in range(0, CP, 8):
            part = pl.ds(c, 8)
            below = [source[t, start - 1, part] for t in range(3)]
            here = [source[t, start, part] for t in range(3)]
            for k in range(unroll):
                r = start + k
                above = [source[t, r + 1, part] for t in range(3)]
                to_east, to_west = east_of(here), west_of(here)
                for t in range(3):
                    target[t, r, part] = (
                        (rhs[t, r, part] + w_n[t, r, part] * above[t])
                        + (w_s[t, r, part] * below[t] + w_e[t, r, part] * to_east[t])
                        + w_w[t, r, part] * to_west[t]
                    )
                below, here = here, above
        return carry

    lax.fori_loop(0, (stop - first + unroll - 1) // unroll, block, 0)


def kernel(
    n_lat, n_lon, size, back,
    partner_ref, count_ref, scale_ref, sigma_ref, value_ref, cell_ref, bottom_ref, diffusivity_ref, out_ref, state_ref,
    outgoing, arrived, lhs0, onehot0, lhs1, onehot1, total, field, fits, pieces, picked0, picked1, coef_ref,
    cur, nxt, rhs, inv, w_e, w_w, w_n, w_s, pack_e, pack_w, edge_e, edge_w,
    coef, coef_e, coef_w, fold, coef_fold, mirror,
    local_sem, obs_send, obs_recv, way_send, way_recv, fold_send, fold_recv, relay_send, relay_recv,
    back_send, back_recv,
):
    n = n_lat * n_lon
    lat = lax.axis_index("lat")
    lon = lax.axis_index("lon")
    me = lat * n_lon + lon
    top = lat == n_lat - 1
    load = pltpu.make_async_copy(value_ref, outgoing.at[0:C], local_sem.at[0])
    load.start()
    barrier = pltpu.get_barrier_semaphore()

    def greet(i, carry):
        pl.semaphore_signal(barrier, inc=1, device_id=place_of(lax.rem(me + i, n), n_lon), device_id_type=MESH)
        return carry

    @pl.when(lat == 0)
    def _():
        cur[0:2, 0:DEEP] = jnp.zeros((2, DEEP, CP, 128), F32)
        edge_e[0:2] = jnp.zeros((2, CP, 128), F32)
        edge_w[0:2] = jnp.zeros((2, CP, 128), F32)
        coef[:, :, 0:GRP, :] = jnp.zeros((2, 3, GRP, 128), F32)
        coef_e[:, 0:GRP, :] = jnp.zeros((3, GRP, 128), F32)
        coef_w[:, 0:GRP, :] = jnp.zeros((3, GRP, 128), F32)

    @pl.when(top)
    def _():
        edge_e[8:10] = jnp.zeros((2, CP, 128), F32)
        edge_w[8:10] = jnp.zeros((2, CP, 128), F32)
        coef_e[:, GRP + ROWS : CEXT, :] = jnp.zeros((3, GRP, 128), F32)
        coef_w[:, GRP + ROWS : CEXT, :] = jnp.zeros((3, GRP, 128), F32)

    lax.fori_loop(1, n, greet, 0)
    lane_row = lanes_of((1, 128))

    def mask_cells(o, carry):
        row = cell_ref[pl.ds(o, 1), :]
        outgoing[C, pl.ds(o, 1), :] = jnp.where(lane_row < count_ref[0, o], row, -1).astype(F32)
        return carry

    lax.fori_loop(0, n, mask_cells, 0, unroll=8)
    for t in range(2):
        lanes = slice(t * 128, (t + 1) * 128)
        coef_ref[t, 0] = bottom_ref[:, lanes].astype(F32)
        coef_ref[t, 1] = diffusivity_ref[0, :, lanes]
        coef_ref[t, 2] = diffusivity_ref[1, :, lanes]
        coef[t, :, GRP : GRP + ROWS, :] = coef_ref[t]
    total[...] = jnp.zeros_like(total)
    load.wait()
    pl.semaphore_wait(barrier, n - 1)

    east = lax.rem(lon + 1, n_lon)
    west = lax.rem(lon + n_lon - 1, n_lon)
    has_n = lat < n_lat - 1
    has_s = lat > 0
    everywhere = lat >= 0
    north = jnp.minimum(lat + 1, n_lat - 1)
    south = jnp.maximum(lat - 1, 0)
    ways = [
        (everywhere, lat, east, everywhere),
        (everywhere, lat, west, everywhere),
        (has_n, north, lon, has_s),
        (has_n, north, east, has_s),
        (has_n, north, west, has_s),
        (has_s, south, lon, has_n),
        (has_s, south, east, has_n),
        (has_s, south, west, has_n),
    ]
    mid_g, low_g, high_g = pl.ds(GRP, ROWS), pl.ds(0, GRP), pl.ds(GRP + ROWS, GRP)
    head, tail = pl.ds(0, GRP), pl.ds(ROWS - GRP, GRP)
    copies = [
        ((pack_e, edge_w.at[pl.ds(2, 6)]), (coef_ref.at[1], coef_w.at[:, mid_g, :])),
        ((pack_w, edge_e.at[pl.ds(2, 6)]), (coef_ref.at[0], coef_e.at[:, mid_g, :])),
        (
            (field.at[:, pl.ds(ROWS - DEEP, DEEP)], cur.at[pl.ds(0, 2), pl.ds(0, DEEP)]),
            (coef_ref.at[:, :, tail, :], coef.at[:, :, low_g, :]),
        ),
        ((pack_e.at[pl.ds(4, 2)], edge_w.at[pl.ds(0, 2)]), (coef_ref.at[1, :, tail, :], coef_w.at[:, low_g, :])),
        ((pack_w.at[pl.ds(4, 2)], edge_e.at[pl.ds(0, 2)]), (coef_ref.at[0, :, tail, :], coef_e.at[:, low_g, :])),
        (
            (field.at[:, pl.ds(0, DEEP)], cur.at[pl.ds(0, 2), pl.ds(EXT - DEEP, DEEP)]),
            (coef_ref.at[:, :, head, :], coef.at[:, :, high_g, :]),
        ),
        ((pack_e.at[pl.ds(0, 2)], edge_w.at[pl.ds(8, 2)]), (coef_ref.at[1, :, head, :], coef_w.at[:, high_g, :])),
        ((pack_w.at[pl.ds(0, 2)], edge_e.at[pl.ds(8, 2)]), (coef_ref.at[0, :, head, :], coef_e.at[:, high_g, :])),
    ]

    def copy_of(w, k):
        source, target = copies[w][k]
        return pltpu.make_async_remote_copy(
            src_ref=source,
            dst_ref=target,
            send_sem=way_send.at[w, k],
            recv_sem=way_recv.at[w, k],
            device_id=(ways[w][1], ways[w][2]),
            device_id_type=MESH,
        )

    def start_ways(k):
        for w in range(8):
            @pl.when(ways[w][0])
            def _():
                copy_of(w, k).start()

    def wait_ways(k, which):
        for w in which:
            @pl.when(ways[w][3])
            def _():
                copy_of(w, k).wait_recv()

    def drain_ways(k):
        for w in range(8):
            @pl.when(ways[w][0])
            def _():
                copy_of(w, k).wait_send()

    planes = n_lat // 2
    share = DEEP // planes
    plane = lat // 2
    relays = lax.rem(lat, 2) == 1
    mine = pl.ds(2 * lon, 2)

    def lon_copy(k, i):
        source, target = ((fold.at[mine], fold), (coef_ref.at[:, :, tail, :], coef_fold))[k]
        return pltpu.make_async_remote_copy(
            src_ref=source,
            dst_ref=target.at[mine],
            send_sem=fold_send.at[k, i],
            recv_sem=fold_recv.at[k, i],
            device_id=(lat, lax.rem(lon + i, n_lon)),
            device_id_type=MESH,
        )

    def start_lon(k):
        def one(i, carry):
            lon_copy(k, i).start()
            return carry

        lax.fori_loop(1, n_lon, one, 0)

    def wait_lon(k):
        def one(i, carry):
            lon_copy(k, i).wait()
            return carry

        lax.fori_loop(1, n_lon, one, 0)

    def share_of(x):
        return field.at[:, pl.ds(ROWS - DEEP + share * x, share)]

    def to_relay(x):
        return pltpu.make_async_remote_copy(
            src_ref=share_of(x),
            dst_ref=fold.at[mine],
            send_sem=relay_send.at[0, x],
            recv_sem=relay_recv.at[0, 0],
            device_id=(2 * x + 1, lon),
            device_id_type=MESH,
        )

    def from_relay(x):
        return pltpu.make_async_remote_copy(
            src_ref=mirror,
            dst_ref=cur.at[:, pl.ds(EXT - share * (x + 1), share)],
            send_sem=relay_send.at[1, 0],
            recv_sem=relay_recv.at[1, x],
            device_id=(n_lat - 1, lon),
            device_id_type=MESH,
        )

    def own_share():
        return pltpu.make_async_copy(share_of(planes - 1), fold.at[mine], local_sem.at[1])

    def relay_out():
        @pl.when(top)
        def _():
            for x in range(planes - 1):
                to_relay(x).start()
            own_share().start()
            own_share().wait()

        @pl.when(jnp.logical_and(relays, lat < n_lat - 1))
        def _():
            to_relay(0).wait_recv()

        @pl.when(relays)
        def _():
            start_lon(0)

    def relay_back():
        @pl.when(relays)
        def _():
            wait_lon(0)
            for d in range(share):
                tiles = mirrored(lambda p: fold[p, share - 1 - d], CP)
                for t in range(3):
                    mirror[t, d] = tiles[t]

        for x in range(planes - 1):
            @pl.when(jnp.logical_and(relays, plane == x))
            def _():
                from_relay(x).start()

        @pl.when(top)
        def _():
            own = pltpu.make_async_copy(mirror, cur.at[:, pl.ds(EXT - DEEP, share)], local_sem.at[1])
            own.start()
            own.wait()
            for x in range(planes - 1):
                to_relay(x).wait_send()

    def relay_end():
        @pl.when(top)
        def _():
            for x in range(planes - 1):
                from_relay(x).wait_recv()

        for x in range(planes - 1):
            @pl.when(jnp.logical_and(relays, plane == x))
            def _():
                from_relay(x).wait_send()

    corner = partner_ref[0]
    tile0 = corner // 128
    shift = lax.rem(corner, 128)
    places = [lax.rem(tile0 + x - 4 + 2 * n_lon, 2 * n_lon) for x in range(1, 6)]

    def mirrored(load, rows):
        lane = lanes_of((rows, 128))
        index = (shift - lane) & 127
        near = lane <= shift
        tiles = [jnp.take_along_axis(load(p), index, axis=1) for p in places]
        merged = [jnp.where(near, tiles[x], tiles[x - 1]) for x in range(1, 5)]
        return merged[2], merged[1], jnp.where(lane < 64, merged[0], merged[3])

    start_ways(1)

    @pl.when(top)
    def _():
        start_lon(1)
        own = pltpu.make_async_copy(coef_ref.at[:, :, tail, :], coef_fold.at[mine], local_sem.at[1])
        own.start()
        own.wait()

    def send(i, carry):
        owner = lax.rem(me + i, n)
        pltpu.make_async_remote_copy(
            src_ref=outgoing.at[:, owner, :],
            dst_ref=arrived.at[i, 0 : C + 1, :],
            send_sem=obs_send,
            recv_sem=obs_recv.at[i // (2 * size)],
            device_id=place_of(owner, n_lon),
            device_id_type=MESH,
        ).start()
        return carry

    early = n // 4
    beside = n // 2
    rest = n - early - beside

    own_obs = pltpu.make_async_copy(outgoing.at[:, me, :], arrived.at[0, 0 : C + 1, :], local_sem.at[0])
    own_obs.start()
    lax.fori_loop(1, early, send, 0)

    wait_ways(1, range(8))
    side_c = lanes_of((3, CEXT, 128)) < 64
    coef_e[...] = jnp.where(side_c, coef_e[...], coef_w[...])

    @pl.when(top)
    def _():
        wait_lon(1)
        for k in range(3):
            tiles = mirrored(lambda p: coef_fold[p, k], GRP)
            for d in range(GRP):
                row = GRP + ROWS + d
                for t in range(2):
                    coef[t, k, row : row + 1, :] = tiles[t][GRP - 1 - d : GRP - d]
                coef_e[k, row : row + 1, :] = tiles[2][GRP - 1 - d : GRP - d]

    channel = lax.broadcasted_iota(jnp.int32, (CP, 128), 0)
    level = jnp.where(channel < LEV, channel, jnp.where(channel < 2 * LEV, channel - LEV, 0))
    level = jnp.where(channel < C, level, 2 * LEV).astype(F32)
    scale = jnp.zeros((CP, 128), F32)
    sigma = jnp.zeros((CP, 128), F32)
    for c in range(C):
        scale = jnp.where(channel == c, scale_ref[c], scale)
        sigma = jnp.where(channel == c, sigma_ref[c], sigma)

    def coef_row(k, row):
        return [
            jnp.broadcast_to(ref[k, pl.ds(row, 1), :], (CP, 128))
            for ref in (coef.at[0], coef.at[1], coef_e)
        ]

    def weigh(r, carry):
        g = r + (GRP - DEEP)
        deep, deep_n, deep_s = coef_row(0, g), coef_row(0, g + 1), coef_row(0, g - 1)
        k0 = coef_row(1, g)
        k1, k1_n, k1_s = coef_row(2, g), coef_row(2, g + 1), coef_row(2, g - 1)
        k0_east, k0_west = east_of(k0), west_of(k0)
        deep_east, deep_west = east_of(deep), west_of(deep)
        for t in range(3):
            def face(k, deep_there):
                both = level < jnp.minimum(deep[t], deep_there)
                return jnp.where(both, scale * (0.5 * k), 0.0)

            e = face(k0[t] + k0_east[t], deep_east[t])
            w = face(k0[t] + k0_west[t], deep_west[t])
            m = face(k1[t] + k1_n[t], deep_n[t])
            s = face(k1[t] + k1_s[t], deep_s[t])
            over = 1.0 / (1.0 + e + w + m + s)
            inv[t, r] = over
            w_e[t, r] = e * over
            w_w[t, r] = w * over
            w_n[t, r] = m * over
            w_s[t, r] = s * over
        return carry

    def weigh_and_send(r, carry):
        send(early + r, carry)
        return weigh(r, carry)

    lax.fori_loop(0, beside, weigh_and_send, 0)
    lax.fori_loop(beside, EXT, weigh, 0)
    drain_ways(1)

    def arrive(group, first):
        window = arrived.at[pl.ds(group * 2 * size + first, 2 * size - first), 0 : C + 1, :]
        pltpu.make_async_copy(window, window, obs_recv.at[group]).wait()

    pairs = n // size // 2
    dims = (((1,), (1,)), ((), ()))
    batch = -(-rest // (pairs - 1))

    def accumulate(lhs, onehot):
        total[...] += lax.dot_general(lhs[...], onehot[...], dims, preferred_element_type=F32)

    own_obs.wait()
    arrive(0, 1)
    build_chunk(arrived, 0, size, lhs0, onehot0)

    def pair(i, carry):
        first = early + beside + i * batch
        lax.fori_loop(first, jnp.minimum(first + batch, n), send, 0)
        arrive(i + 1, 0)
        build_chunk(arrived, 2 * i + 1, size, lhs1, onehot1)
        accumulate(lhs0, onehot0)
        build_chunk(arrived, 2 * i + 2, size, lhs0, onehot0)
        accumulate(lhs1, onehot1)
        return carry

    lax.fori_loop(0, pairs - 1, pair, 0)
    build_chunk(arrived, 2 * pairs - 1, size, lhs1, onehot1)
    accumulate(lhs0, onehot0)
    accumulate(lhs1, onehot1)
    for b in range(BAND):
        first = b * 2 * CP
        band = total[first : first + CP, :] + total[first + CP : first + 2 * CP, :]
        for t in range(4):
            field[t % 2, 2 * b + t // 2] = band[:, t * 128 : (t + 1) * 128]

    lane16 = lanes_of((CP, 128)) >> 4
    for i in range(ROWS // 8):
        first = jnp.zeros((CP, 128), F32)
        last = jnp.zeros((CP, 128), F32)
        for j in range(8):
            x = field[0, 8 * i + j]
            y = field[1, 8 * i + j]
            first = jnp.where(lane16 == j, pltpu.roll(x, 16 * j, 1) if j else x, first)
            last = jnp.where(lane16 == j, pltpu.roll(y, 16 * j + 16, 1) if j < 7 else y, last)
        pack_w[i] = first
        pack_e[i] = last

    start_ways(0)

    relay_out()

    def begin(r, tiles):
        deep = coef_row(0, r + (GRP - DEEP))
        for t in range(3):
            start = jnp.where(level < deep[t], tiles[t] * sigma, 0.0)
            cur[t, r] = start
            rhs[t, r] = start * inv[t, r]

    side = lanes_of((CP, 128)) < 64

    def unpack(i):
        from_e = edge_e[i]
        from_w = edge_w[i]
        for j in range(8):
            x = pltpu.roll(from_e, 128 - 16 * j, 1) if j else from_e
            y = pltpu.roll(from_w, 112 - 16 * j, 1) if j < 7 else from_w
            row = 8 * i + j - (GRP - DEEP)
            if 0 <= row < EXT:
                cur[2, row] = jnp.where(side, x, y)

    def begin_own(r, carry):
        begin(r, [field[0, r - DEEP], field[1, r - DEEP], cur[2, r]])
        return carry

    def begin_ghost(r, carry):
        begin(r, [cur[t, r] for t in range(3)])
        return carry

    wait_ways(0, range(0, 5))
    for i in range(0, 8):
        unpack(i)
    lax.fori_loop(0, DEEP, begin_ghost, 0)
    lax.fori_loop(DEEP, DEEP + ROWS, begin_own, 0, unroll=2)

    weights = (w_e, w_w, w_n, w_s)
    def renew(first, stop):
        def one(r, carry):
            for t in range(3):
                rhs[t, r] = cur[t, r] * inv[t, r]
            return carry

        lax.fori_loop(first, stop, one, 0, unroll=2)

    def sweeps(step, low, high):
        def two(p, carry):
            for half in range(2):
                k = step * SWEEPS + 2 * p + 1 + half
                sweep((cur, nxt)[half], (nxt, cur)[half], rhs, weights, low(k), high(k), 12)
            return carry

        lax.fori_loop(0, SWEEPS // 2, two, 0)

    limit = DEEP + ROWS
    reach = lambda k: limit - k
    sweeps(0, lambda k: k, reach)
    relay_back()
    renew(SWEEPS + 1, reach(SWEEPS + 1))
    sweeps(1, lambda k: k, reach)

    wait_ways(0, range(5, 8))

    @pl.when(has_n)
    def _():
        for i in range(8, 10):
            unpack(i)

    relay_end()
    lax.fori_loop(limit, EXT, begin_ghost, 0)
    sweeps(0, reach, lambda k: EXT - k)
    renew(reach(SWEEPS + 1), EXT - SWEEPS - 1)
    sweeps(1, reach, lambda k: EXT - k)

    for b in range(0, BAND, 4):
        for t in range(2):
            values = [cur[t, 2 * b + k + DEEP] * sigma for k in range(8)]
            across = jnp.swapaxes(jnp.stack(values, axis=0), 0, 1)
            state_ref[:, 2 * b : 2 * b + 8, t * 128 : (t + 1) * 128] = across[:C]
            for half in range(2):
                first = half * COLS + t * 128
                for k in range(2):
                    rows = jnp.concatenate([values[4 * k + half], values[4 * k + 2 + half]], axis=0)
                    high = rows.astype(BF16)
                    low = (rows - high.astype(F32)).astype(BF16)
                    here = pl.ds((b + 2 * k) * CP, 2 * CP)
                    pieces[here, first : first + 128] = high
                    pieces[here, PLACES + first : PLACES + first + 128] = low

    def multiply(g, onehot, picked):
        for j in range(back):
            _, halves = split(arrived[g * back + j, C : C + 1, :])
            store_onehot(onehot, halves, slice(j * 128, (j + 1) * 128))
        hot = onehot[:, : back * 128]
        picked[...] = jnp.dot(pieces[:, :PLACES], hot, preferred_element_type=F32) + jnp.dot(
            pieces[:, PLACES:], hot, preferred_element_type=F32
        )

    def pick(g, picked):
        for j in range(back):
            band, _ = split(arrived[g * back + j, C : C + 1, :])
            band = jnp.broadcast_to(band, (CP, 128))
            fit = jnp.zeros((CP, 128), F32)
            for b in range(BAND):
                fit += jnp.where(band == b, picked[b * CP : (b + 1) * CP, j * 128 : (j + 1) * 128], 0.0)
            fits[g * back + j] = fit

    def give_back(i):
        pltpu.make_async_remote_copy(
            src_ref=fits.at[i, 0:C, :],
            dst_ref=out_ref.at[:, me, :],
            send_sem=back_send,
            recv_sem=back_recv,
            device_id=place_of(lax.rem(me - i + n, n), n_lon),
            device_id_type=MESH,
        ).start()

    def hand(g):
        @pl.when(g > 0)
        def _():
            give_back(g * back)

        for j in range(1, back):
            give_back(g * back + j)

    multiply(0, onehot0, picked0)

    def turn(i, carry):
        multiply(2 * i + 1, onehot1, picked1)
        pick(2 * i, picked0)
        multiply(2 * i + 2, onehot0, picked0)
        pick(2 * i + 1, picked1)
        hand(2 * i)
        hand(2 * i + 1)
        return carry

    turns = n // back // 2
    lax.fori_loop(0, turns - 1, turn, 0)
    multiply(2 * turns - 1, onehot1, picked1)
    pick(2 * turns - 2, picked0)
    hand(2 * turns - 2)
    pick(2 * turns - 1, picked1)
    hand(2 * turns - 1)
    own_fit = pltpu.make_async_copy(fits.at[0, 0:C, :], out_ref.at[:, me, :], local_sem.at[0])
    own_fit.start()
    own_fit.wait()
    drain_ways(0)
    sent = arrived.at[1:n, 0 : C + 1, :]
    pltpu.make_async_copy(sent, sent, obs_send).wait()
    sent = fits.at[1:n, 0:C, :]
    pltpu.make_async_copy(sent, sent, back_send).wait()
    pltpu.make_async_copy(sent, sent, back_recv).wait()


def run(n_lat, n_lon, partner, count, scale, sigma, value, cell, bottom_level, diffusivity):
    n = n_lat * n_lon
    size = min(8, n // 4)
    back = min(4, n // 4)
    planes = n_lat // 2
    vmem = pl.BlockSpec(memory_space=pltpu.VMEM)
    buffers = [
        pltpu.VMEM((BAND * 2 * CP, size * 128), BF16),
        pltpu.VMEM((PLACES, size * 128), BF16),
    ]
    state = pltpu.VMEM((3, EXT, CP, 128), F32)
    return pl.pallas_call(
        functools.partial(kernel, n_lat, n_lon, size, back),
        out_shape=(
            jax.ShapeDtypeStruct((C, n, 128), F32),
            jax.ShapeDtypeStruct((C, ROWS, COLS), F32),
        ),
        in_specs=[
            *[pl.BlockSpec(memory_space=pltpu.SMEM)] * 4,
            pl.BlockSpec(memory_space=pl.ANY),
            vmem,
            vmem,
            vmem,
        ],
        out_specs=(vmem, vmem),
        scratch_shapes=[
            pltpu.VMEM((C + 1, n, 128), F32),
            pltpu.VMEM((n, CP, 128), F32),
            *buffers,
            *buffers,
            pltpu.VMEM((BAND * 2 * CP, PLACES), F32),
            pltpu.VMEM((2, ROWS, CP, 128), F32),
            pltpu.VMEM((n, CP, 128), F32),
            pltpu.VMEM((BAND * CP, 2 * PLACES), BF16),
            pltpu.VMEM((BAND * CP, back * 128), F32),
            pltpu.VMEM((BAND * CP, back * 128), F32),
            pltpu.VMEM((2, 3, ROWS, 128), F32),
            *[state] * 8,
            pltpu.VMEM((ROWS // 8, CP, 128), F32),
            pltpu.VMEM((ROWS // 8, CP, 128), F32),
            pltpu.VMEM((CEXT // 8, CP, 128), F32),
            pltpu.VMEM((CEXT // 8, CP, 128), F32),
            pltpu.VMEM((2, 3, CEXT, 128), F32),
            pltpu.VMEM((3, CEXT, 128), F32),
            pltpu.VMEM((3, CEXT, 128), F32),
            pltpu.VMEM((2 * n_lon, DEEP // planes, CP, 128), F32),
            pltpu.VMEM((2 * n_lon, 3, GRP, 128), F32),
            pltpu.VMEM((3, DEEP // planes, CP, 128), F32),
            pltpu.SemaphoreType.DMA((2,)),
            pltpu.SemaphoreType.DMA,
            pltpu.SemaphoreType.DMA((n // size // 2,)),
            pltpu.SemaphoreType.DMA((8, 2)),
            pltpu.SemaphoreType.DMA((8, 2)),
            pltpu.SemaphoreType.DMA((2, n_lon)),
            pltpu.SemaphoreType.DMA((2, n_lon)),
            pltpu.SemaphoreType.DMA((2, planes)),
            pltpu.SemaphoreType.DMA((2, planes)),
            pltpu.SemaphoreType.DMA,
            pltpu.SemaphoreType.DMA,
        ],
        compiler_params=pltpu.CompilerParams(
            collective_id=0, has_side_effects=True, vmem_limit_bytes=VMEM_LIMIT
        ),
        name="covariance",
    )(partner, count, scale, sigma, value, cell, bottom_level, diffusivity)


def per_device(
    n_lat, n_lon, obs_value, obs_cell, obs_count, bottom_level, diffusivity, partner, length_scale, sigma
):
    fit, diffused = run(
        n_lat, n_lon, partner, obs_count, length_scale, sigma, obs_value[0], obs_cell[0], bottom_level, diffusivity
    )
    return fit[None], diffused


def solution(mesh):
    n_lat, n_lon = mesh.shape["lat"], mesh.shape["lon"]
    return jax.shard_map(
        functools.partial(per_device, n_lat, n_lon),
        mesh=mesh,
        in_specs=(
            P(("lat", "lon"), None, None, None),
            P(("lat", "lon"), None, None),
            P(("lat", "lon"), None),
            P("lat", "lon"),
            P(None, "lat", "lon"),
            P("lon"),
            P(),
            P(),
        ),
        out_specs=(P(("lat", "lon"), None, None, None), P(None, "lat", "lon")),
        check_vma=False,
    )
```
